256 devices in a mesh: seq: 32 (over z, x), feat: 8 (over y, core).
Axes of the slice: x: 4, y: 4, z: 8, core: 2. Of those that a mesh axis runs over, the one named last changes fastest.
Arguments:
- teacher_states: bfloat16 [4, 32768, 3584], P(None, 'seq', 'feat')
- student_states: bfloat16 [32768, 2304], P('seq'), may hold values from -6 to 6
- projection: bfloat16 [4, 2304, 3584], P(None, 'seq', 'feat'), may hold values from -0.125 to 0.125
- layer_pick: int32 [4], replicated, may hold values from 0 to 3, each once
- validity: int32 [32768], P('seq'), may hold values from 0 to 1, as said below
Outputs:
- whitened_error: bfloat16 [4, 32768, 3584], P(None, 'seq', 'feat')
- total_loss: float32 [], replicated
The draws below stay inside these ranges and needn't reach their ends.
Inputs may be any that keep to these rules, and one draw needn't show every extreme that they name: `validity`: the positions form 2 sequences of 16384 positions each; in each sequence a prefix of 4096 positions or more is 1 and the rest is 0.
All inputs are finite; a program needn't handle non-finite values.
Results may differ from the reference program's by a relative error of at most 0.00045.
Values may be sent and summed in bfloat16 or wider, within the bound.
No kernel may reach another device: no remote copies, remote signals or barrier semaphores. Data moves between devices by JAX's collectives and lax.ppermute only.
A program may use at most 64 MiB of HBM per device.

```python
import math
import jax
import jax.numpy as jnp
from jax import lax

D = 3584
DS = 2304
LAYERS = 4
SEQS = 2
TOKENS = 32768


def draw_teacher_states(key, part):
    subkeys = jax.random.split(jax.random.fold_in(key, 101), 4)
    column = jnp.exp(jax.random.uniform(subkeys[0], (LAYERS, 1, D), jnp.float32) * math.log(10.0))
    offset = jax.random.normal(subkeys[1], (LAYERS, 1, D), jnp.float32) * 2.0
    position = jnp.arange(TOKENS, dtype=jnp.float32) / TOKENS
    jitter = jax.random.uniform(subkeys[2], (1, TOKENS, 1), jnp.float32, -0.3, 0.3)
    fluctuation = jax.random.normal(subkeys[3], (LAYERS, TOKENS, D), jnp.float32)
    row_scale = (1.0 + 2.0 * position)[None, :, None] * jnp.exp(jitter)
    return (column * (offset + row_scale * fluctuation)).astype(jnp.bfloat16)


def draw_validity(key, part):
    seq_length = TOKENS // SEQS
    lengths = jax.random.randint(jax.random.fold_in(key, 23), (SEQS,), seq_length // 4, seq_length + 1)
    position = jnp.arange(TOKENS, dtype=jnp.int32) % seq_length
    limits = jnp.repeat(lengths, seq_length)
    return (position < limits).astype(jnp.int32)


def block_levels(key, extent, shards, smallest, high):
    def one(axis_at, parts):
        heights = jax.random.uniform(jax.random.fold_in(jax.random.fold_in(key, 6), axis_at), (parts,), jnp.float32, smallest / len(shards), high / len(shards))
        return jnp.repeat(jnp.exp(heights), extent[axis_at] // parts).reshape((-1,) + (1,) * (len(extent) - axis_at - 1))

    level = one(*shards[0])
    for cut in shards[1:]:
        level = level * one(*cut)
    return level


def scatter_about(key, extent, width, limit, pieces=(), kind=jnp.bfloat16):
    entries = width * jax.random.normal(key, extent, jnp.float32)
    if pieces:
        entries = entries * block_levels(key, extent, pieces, -0.22, 0.18)
    return jnp.clip(entries, -limit, limit).astype(kind)


def setup_inputs(seed: int = 0) -> dict:
    key_of = jax.random.split(jax.random.key(seed), 6)
    return {
        "teacher_states": draw_teacher_states(jax.random.fold_in(key_of[5], 71), 0),
        "student_states": scatter_about(key_of[1], (TOKENS, DS), 1.0, 6.0, ((0, 32),)),
        "projection": scatter_about(key_of[2], (LAYERS, DS, D), DS ** -0.5, 0.125, ((1, 32), (2, 8))),
        "layer_pick": jax.random.permutation(key_of[3], LAYERS).astype(jnp.int32),
        "validity": draw_validity(jax.random.fold_in(key_of[5], 71), 0),
    }


epsilon = 1e-05

def reference(teacher_states, student_states, projection, layer_pick, validity):
    weighting = validity.astype(jnp.float32)
    counted = jnp.sum(weighting)
    squared_total = jnp.zeros((), jnp.float32)
    errors = []
    for number in range(LAYERS):
        chosen = jnp.take(teacher_states, layer_pick[number], axis=0).astype(jnp.float32)
        average = lax.optimization_barrier(jnp.sum(chosen * weighting[:, None], axis=0)) / counted
        centred = chosen - average
        variance = lax.optimization_barrier(jnp.sum(weighting[:, None] * centred * centred, axis=0)) / counted
        target = centred / jnp.sqrt(variance + epsilon)
        predicted = jnp.dot(student_states, projection[number], preferred_element_type=jnp.float32)
        residual = predicted - target
        errors.append((weighting[:, None] * residual).astype(jnp.bfloat16))
        squared_total = squared_total + jnp.sum(weighting[:, None] * residual * residual)
    total_loss = squared_total / (counted * D * LAYERS)
    return (jnp.stack(errors), total_loss)
```

```python
import jax
import jax.numpy as jnp
from jax import lax
from jax.experimental import pallas as pl
from jax.experimental.pallas import tpu as pltpu
from jax.sharding import Mesh
from jax.sharding import PartitionSpec as P

D = 3584
LAYERS = 4
SEQ = ("seq_0", "seq_1")
FEAT = ("feat_0", "feat_1")
ALL = SEQ + FEAT
NZ, NX = 8, 4
epsilon = 1e-05

C_COLS = 768
HALF = 512
BN = 256
VMEM = 56 * 1024 * 1024

Z_ORDER = (0, 1, -1, 2, -2, 3, -3, 4)
X_ORDER = (0, 1, -1, 2)
NEAR = 3
f32 = jnp.float32
bf16 = jnp.bfloat16


def shift(value, axis, size, by):
    return lax.ppermute(value, axis, [(i, (i - by) % size) for i in range(size)])


def from_z(value, by):
    return shift(value, "seq_0", NZ, by)


def from_x(value, by):
    return shift(value, "seq_1", NX, by)


def params(**kw):
    return pltpu.CompilerParams(vmem_limit_bytes=VMEM, **kw)


def moments_kernel(pick, teacher, weight, chosen, stats):
    x16 = teacher[0]
    chosen[0] = x16
    x = x16.astype(f32)
    w = weight[...]
    count = jnp.sum(w, axis=1, keepdims=True)
    mean = jnp.sum(x * w, axis=1, keepdims=True) / jnp.maximum(count, 1.0)
    centred = x - mean
    spread = jnp.sum(w * centred * centred, axis=1, keepdims=True)
    lane = lax.broadcasted_iota(jnp.int32, (x.shape[0], 128), 1)
    table = jnp.where(lane == 0, mean, jnp.where(lane == 1, spread, count))
    stats[0] = table.T[:8]


def local_moments(teacher, weight, pick):
    layers, features, tokens = teacher.shape
    return pl.pallas_call(
        moments_kernel,
        grid_spec=pltpu.PrefetchScalarGridSpec(
            num_scalar_prefetch=1,
            grid=(layers,),
            in_specs=[
                pl.BlockSpec((1, features, tokens), lambda i, p: (p[i], 0, 0)),
                pl.BlockSpec((1, tokens), lambda i, p: (0, 0)),
            ],
            out_specs=[
                pl.BlockSpec((1, features, tokens), lambda i, p: (i, 0, 0)),
                pl.BlockSpec((1, 8, features), lambda i, p: (i, 0, 0)),
            ],
        ),
        out_shape=[
            jax.ShapeDtypeStruct((layers, features, tokens), bf16),
            jax.ShapeDtypeStruct((layers, 8, features), f32),
        ],
        compiler_params=params(),
        cost_estimate=pl.CostEstimate(flops=20_000_000, bytes_accessed=8_000_000, transcendentals=0),
        name="moments",
    )(pick, teacher, weight)


def merge(former, latter):
    first_mean, first_spread, first_count = former[:, 0], former[:, 1], former[:, 2]
    second_mean, second_spread, second_count = latter[:, 0], latter[:, 1], latter[:, 2]
    joined = first_count + second_count
    share = second_count / jnp.maximum(joined, 1.0)
    delta = second_mean - first_mean
    mean = first_mean + delta * share
    spread = first_spread + second_spread + delta * delta * first_count * share
    row = lax.broadcasted_iota(jnp.int32, former.shape, 1)
    return jnp.where(row == 0, mean[:, None], jnp.where(row == 1, spread[:, None], joined[:, None]))


def order_kernel(zs, xs, student, near, far):
    i = pl.program_id(0)

    @pl.when(i < NEAR)
    def _():
        for j in range(NX):
            near[j, 0] = student[0, xs[j]]

    @pl.when(i >= NEAR)
    def _():
        for j in range(NX):
            far[j, 0] = student[0, xs[j]]


def in_order(student, zs, xs):
    nz, nx, rows, tokens = student.shape
    return pl.pallas_call(
        order_kernel,
        grid_spec=pltpu.PrefetchScalarGridSpec(
            num_scalar_prefetch=2,
            grid=(nz,),
            in_specs=[pl.BlockSpec((1, nx, rows, tokens), lambda i, z, x: (z[i], 0, 0, 0))],
            out_specs=[
                pl.BlockSpec((nx, 1, rows, tokens), lambda i, z, x: (0, jnp.minimum(i, NEAR - 1), 0, 0)),
                pl.BlockSpec((nx, 1, rows, tokens), lambda i, z, x: (0, jnp.maximum(i - NEAR, 0), 0, 0)),
            ],
        ),
        out_shape=[
            jax.ShapeDtypeStruct((nx, NEAR, rows, tokens), bf16),
            jax.ShapeDtypeStruct((nx, nz - NEAR, rows, tokens), bf16),
        ],
        compiler_params=params(),
        cost_estimate=pl.CostEstimate(flops=0, bytes_accessed=10_000_000, transcendentals=0),
        name="student_order",
    )(zs, xs, student)


def times(weights, student):
    return lax.dot_general(weights, student, (((0,), (0,)), ((), ())), preferred_element_type=f32)


def finish(predicted, chosen, scale, weight, error):
    target = (chosen[...].astype(f32) - scale[:, 0:1]) * scale[:, 1:2]
    residual = predicted - target
    masked = weight[...] * residual
    error[...] = masked.astype(bf16)
    return jnp.sum(masked * residual, axis=0, keepdims=True)


def whole_kernel(weights, student, chosen, scale, weight, error, loss):
    @pl.when(pl.program_id(0) == 0)
    def _():
        loss[...] = jnp.zeros_like(loss)

    loss[...] += finish(times(weights[...], student[...]), chosen, scale, weight, error)


def whole_product(weights, student, chosen, scale, weight):
    k, cols = weights.shape
    rows, tokens = chosen.shape
    return pl.pallas_call(
        whole_kernel,
        grid=(cols // BN,),
        in_specs=[
            pl.BlockSpec((k, BN), lambda i: (0, i)),
            pl.BlockSpec((k, tokens), lambda i: (0, 0)),
            pl.BlockSpec((BN, tokens), lambda i: (i, 0)),
            pl.BlockSpec((BN, 2), lambda i: (i, 0)),
            pl.BlockSpec((1, tokens), lambda i: (0, 0)),
        ],
        out_specs=[
            pl.BlockSpec((BN, tokens), lambda i: (i, 0)),
            pl.BlockSpec((1, tokens), lambda i: (0, 0)),
        ],
        out_shape=[
            jax.ShapeDtypeStruct((rows, tokens), bf16),
            jax.ShapeDtypeStruct((1, tokens), f32),
        ],
        compiler_params=params(),
        cost_estimate=pl.CostEstimate(flops=2 * k * cols * tokens, bytes_accessed=14_000_000, transcendentals=0),
        name="whole_product",
    )(weights, student, chosen, scale, weight)


def part_kernel(n, has_total, *refs):
    total = refs[-1]
    acc = refs[2 * n][...] if has_total else None
    for k in range(n):
        term = times(refs[k][...], refs[n + k][0])
        acc = term if acc is None else acc + term
    total[...] = acc


def part_product(weights, students, total=None):
    n = len(weights)
    cols = weights[0].shape[1]
    tokens = students[0][0].shape[2]
    in_specs = [pl.BlockSpec((w.shape[0], BN), lambda i: (0, i)) for w in weights]
    in_specs += [pl.BlockSpec((1, *s.shape[1:]), lambda i, j=j: (j, 0, 0)) for s, j in students]
    args = list(weights) + [s for s, _ in students]
    if total is not None:
        in_specs.append(pl.BlockSpec((BN, tokens), lambda i: (i, 0)))
        args.append(total)
    depth = sum(w.shape[0] for w in weights)
    return pl.pallas_call(
        lambda *refs: part_kernel(n, total is not None, *refs),
        grid=(cols // BN,),
        in_specs=in_specs,
        out_specs=pl.BlockSpec((BN, tokens), lambda i: (i, 0)),
        out_shape=jax.ShapeDtypeStruct((cols, tokens), f32),
        input_output_aliases={} if total is None else {len(args) - 1: 0},
        compiler_params=params(),
        cost_estimate=pl.CostEstimate(flops=2 * depth * cols * tokens, bytes_accessed=12_000_000, transcendentals=0),
        name="part_product",
    )(*args)


def last_kernel(left_blocks, steps, left, right, student, total, chosen, scale, weight, loss_in, error_in, error, loss, sums):
    i = pl.program_id(0)

    @pl.when(i == 0)
    def _():
        sums[...] = loss_in[...]

    weights = jnp.where(i < left_blocks, left[...], right[...])
    predicted = total[...] + times(weights, student[0])
    sums[...] += finish(predicted, chosen, scale, weight, error)

    @pl.when(i == steps - 1)
    def _():
        loss[...] = jnp.broadcast_to(jnp.sum(sums[...], axis=1, keepdims=True), loss.shape)


def last_product(left, right, student, index, total, chosen, scale, weight, loss_in, error_in, copies):
    k, tokens = student.shape[1:]
    lefts, rights = left.shape[1] // BN, right.shape[1] // BN
    first = C_COLS // BN
    steps = lefts + rights
    return pl.pallas_call(
        lambda *refs: last_kernel(lefts, steps, *refs),
        grid=(steps,),
        in_specs=[
            pl.BlockSpec((k, BN), lambda i: (0, jnp.minimum(i, lefts - 1))),
            pl.BlockSpec((k, BN), lambda i: (0, jnp.maximum(i - lefts, 0))),
            pl.BlockSpec((1, k, tokens), lambda i: (index, 0, 0)),
            pl.BlockSpec((BN, tokens), lambda i: (i, 0)),
            pl.BlockSpec((BN, tokens), lambda i: (i + first, 0)),
            pl.BlockSpec((BN, 2), lambda i: (i + first, 0)),
            pl.BlockSpec((1, tokens), lambda i: (0, 0)),
            pl.BlockSpec((1, tokens), lambda i: (0, 0)),
            pl.BlockSpec(memory_space=pl.ANY),
        ],
        out_specs=[
            pl.BlockSpec((BN, tokens), lambda i: (i + first, 0)),
            pl.BlockSpec((copies, 128), lambda i: (0, 0)),
        ],
        out_shape=[
            jax.ShapeDtypeStruct(error_in.shape, bf16),
            jax.ShapeDtypeStruct((copies, 128), f32),
        ],
        scratch_shapes=[pltpu.VMEM((1, tokens), f32)],
        input_output_aliases={8: 0},
        compiler_params=params(),
        cost_estimate=pl.CostEstimate(flops=2 * k * steps * BN * tokens, bytes_accessed=12_000_000, transcendentals=0),
        name="last_product",
    )(left, right, student, total, chosen, scale, weight, loss_in, error_in)


def shards(teacher_states, student_states, projection, layer_pick, validity):
    z, x = lax.axis_index("seq_0"), lax.axis_index("seq_1")
    layers, rows, features = projection.shape
    tokens, depth = student_states.shape
    columns = layers * features

    mine = jnp.transpose(projection, (1, 0, 2)).reshape(rows, columns)
    c_mine, b_mine = mine[:, :C_COLS], mine[:, C_COLS:]

    c_next, c_last, c_far = from_x(c_mine, 1), from_x(c_mine, -1), from_x(c_mine, 2)
    ring = {0: b_mine}
    for step in range(1, NZ // 2):
        ring[step] = from_z(ring[step - 1], 1)
        ring[-step] = from_z(ring[1 - step], -1)
    ring[NZ // 2] = from_z(ring[NZ // 2 - 1], 1)

    place = lax.broadcasted_iota(jnp.int32, (NX, 1, 1), 0)
    away = (place - x) % NX
    c_block = jnp.where(
        away == 0, c_mine[None], jnp.where(away == 1, c_next[None], jnp.where(away == 2, c_far[None], c_last[None]))
    ).reshape(NX * rows, C_COLS)
    c_weights = lax.all_gather(c_block, "seq_0", axis=0, tiled=True)

    near = jnp.concatenate([ring[k] for k in Z_ORDER[:NEAR]])
    far = jnp.concatenate([ring[k] for k in Z_ORDER[NEAR:]])

    def along_x(block):
        after, before = from_x(block, 1), from_x(block, -1)
        left, right = from_x(after[:, :HALF], 1), from_x(before[:, HALF:], -1)
        return after, before, left, right

    near_after, near_before, near_left, near_right = along_x(near)
    far_after, far_before, far_left, far_right = along_x(far)

    weight = validity.astype(f32).reshape(1, tokens)
    chosen, stats = local_moments(jnp.transpose(teacher_states, (0, 2, 1)), weight, layer_pick)
    for axis, size in (("seq_1", NX), ("seq_0", NZ)):
        step = 1
        while step < size:
            stats = merge(stats, shift(stats, axis, size, step))
            step *= 2
    counted = stats[0, 2, 0]
    scale = jnp.stack(
        [stats[:, 0].reshape(columns), (1.0 / jnp.sqrt(stats[:, 1] / stats[:, 2] + epsilon)).reshape(columns)], axis=1
    )
    chosen = chosen.reshape(columns, tokens)

    student = student_states.T
    zs = (z + jnp.asarray(Z_ORDER, jnp.int32)) % NZ
    xs = (x + jnp.asarray(X_ORDER, jnp.int32)) % NX
    s_near, s_far = in_order(student.reshape(NZ, NX, rows, tokens), zs, xs)
    s_near, s_far = s_near.reshape(NX, -1, tokens), s_far.reshape(NX, -1, tokens)

    near_across = jnp.concatenate([near_left, near_right], axis=1)
    total = part_product(
        [near, near_after, near_before, near_across, far],
        [(s_near, 0), (s_near, 1), (s_near, 2), (s_near, 3), (s_far, 0)],
    )
    total = part_product([far_after, far_before], [(s_far, 1), (s_far, 2)], total)
    error, loss = whole_product(c_weights, student, chosen, scale, weight)
    copies = NZ * NX * lax.axis_size("feat_0") * lax.axis_size("feat_1")
    error, loss = last_product(
        far_left, far_right, s_far, 3, total, chosen, scale, weight, loss, error, copies
    )
    squares = jnp.sum(lax.all_to_all(loss, ALL, 0, 0, tiled=True)[:, 0])
    total_loss = squares / (counted * D * LAYERS)
    whitened = jnp.transpose(error.reshape(layers, features, tokens), (0, 2, 1))
    return whitened, total_loss


def solution(mesh):
    torus = Mesh(mesh.devices.reshape(NZ, NX, 4, 2), ALL)
    in_specs = (P(None, SEQ, FEAT), P(SEQ, None), P(None, SEQ, FEAT), P(), P(SEQ))
    out_specs = (P(None, SEQ, FEAT), P())
    return jax.shard_map(shards, mesh=torus, in_specs=in_specs, out_specs=out_specs, check_vma=False)
```

```python
import jax
import jax.numpy as jnp
from jax import lax
from jax.experimental import pallas as pl
from jax.experimental.pallas import tpu as pltpu
from jax.sharding import Mesh
from jax.sharding import PartitionSpec as P

D = 3584
LAYERS = 4
SEQ = ("seq_0", "seq_1")
FEAT = ("feat_0", "feat_1")
ALL = SEQ + FEAT
NZ, NX = 8, 4
epsilon = 1e-05

C_COLS = 768
HALF = 512
BN = 256
VMEM = 20 * 1024 * 1024
C_FIRST = True
SC_AFTER = (2, -2, 3, -3)

Z_ORDER = (0, 1, -1, 2, -2, 3, -3, 4)
X_ORDER = (0, 1, -1, 2)
f32 = jnp.float32
bf16 = jnp.bfloat16


def shift(value, axis, size, by):
    return lax.ppermute(value, axis, [(i, (i - by) % size) for i in range(size)])


def from_z(value, by):
    return shift(value, "seq_0", NZ, by)


def from_x(value, by):
    return shift(value, "seq_1", NX, by)


def params(**kw):
    return pltpu.CompilerParams(vmem_limit_bytes=VMEM, **kw)


def stay(value):
    return pltpu.with_memory_space_constraint(value, pltpu.HBM)


def moments_kernel(pick, teacher, weight, chosen, stats):
    x16 = teacher[0]
    chosen[0] = x16
    x = x16.astype(f32)
    w = weight[...]
    count = jnp.sum(w, axis=1, keepdims=True)
    mean = jnp.sum(x * w, axis=1, keepdims=True) / jnp.maximum(count, 1.0)
    centred = x - mean
    spread = jnp.sum(w * centred * centred, axis=1, keepdims=True)
    lane = lax.broadcasted_iota(jnp.int32, (x.shape[0], 128), 1)
    table = jnp.where(lane == 0, mean, jnp.where(lane == 1, spread, count))
    stats[0] = table.T[:8]


def local_moments(teacher, weight, pick):
    layers, features, tokens = teacher.shape
    return pl.pallas_call(
        moments_kernel,
        grid_spec=pltpu.PrefetchScalarGridSpec(
            num_scalar_prefetch=1,
            grid=(layers,),
            in_specs=[
                pl.BlockSpec((1, features, tokens), lambda i, p: (p[i], 0, 0)),
                pl.BlockSpec((1, tokens), lambda i, p: (0, 0)),
            ],
            out_specs=[
                pl.BlockSpec((1, features, tokens), lambda i, p: (i, 0, 0)),
                pl.BlockSpec((1, 8, features), lambda i, p: (i, 0, 0)),
            ],
        ),
        out_shape=[
            jax.ShapeDtypeStruct((layers, features, tokens), bf16),
            jax.ShapeDtypeStruct((layers, 8, features), f32),
        ],
        compiler_params=params(),
        cost_estimate=pl.CostEstimate(flops=20_000_000, bytes_accessed=8_000_000, transcendentals=0),
        name="moments",
    )(pick, stay(teacher), weight)


def merged(groups):
    mean, spread, count = ([g[:, k] for g in groups] for k in range(3))
    joined = sum(count)
    whole = jnp.maximum(joined, 1.0)
    middle = mean[0] + sum(n * (m - mean[0]) for m, n in zip(mean[1:], count[1:])) / whole
    around = sum(spread) + sum(n * (m - middle) * (m - middle) for m, n in zip(mean, count))
    row = lax.broadcasted_iota(jnp.int32, groups[0].shape, 1)
    return jnp.where(row == 0, middle[:, None], jnp.where(row == 1, around[:, None], joined[:, None]))


def place_kernel(zs, *refs):
    *pieces, out = refs
    for k, piece in enumerate(pieces):
        out[zs[k]] = piece[...]


def placed(pieces, zs):
    rows, cols = pieces[0].shape
    n = len(pieces)
    return pl.pallas_call(
        place_kernel,
        in_specs=[pl.BlockSpec(memory_space=pltpu.SMEM)] + [pl.BlockSpec(memory_space=pltpu.VMEM)] * n,
        out_specs=pl.BlockSpec(memory_space=pltpu.VMEM),
        out_shape=jax.ShapeDtypeStruct((n, rows, cols), bf16),
        compiler_params=params(),
        cost_estimate=pl.CostEstimate(flops=0, bytes_accessed=2_500_000, transcendentals=0),
        name="placed",
    )(zs, *pieces).reshape(n * rows, cols)


def columns_kernel(rows, student, out):
    order = [i * NX + j for j in range(NX) for i in range(NZ)]
    out[...] = jnp.concatenate([student[:, pl.ds(k * rows, rows)] for k in order], axis=1)


def by_x(student, rows):
    tokens, depth = student.shape
    block = 256
    return pl.pallas_call(
        lambda *refs: columns_kernel(rows, *refs),
        grid=(tokens // block,),
        in_specs=[pl.BlockSpec((block, depth), lambda i: (i, 0))],
        out_specs=pl.BlockSpec((block, depth), lambda i: (i, 0)),
        out_shape=jax.ShapeDtypeStruct((tokens, depth), bf16),
        compiler_params=params(),
        cost_estimate=pl.CostEstimate(flops=0, bytes_accessed=10_000_000, transcendentals=0),
        name="columns_by_x",
    )(student)


def dot(weights, student):
    return lax.dot_general(weights, student, (((0,), (1,)), ((), ())), preferred_element_type=f32)


def product_kernel(steps, parts, lefts, first, xs, student, *refs):
    if parts == 1:
        weights = refs[0][...]
        refs = refs[1:]
    else:
        *refs, joined = refs
        for k in range(parts - 1):
            joined[xs[k]] = refs[k][...]
        left = pl.program_id(0) < lefts
        joined[xs[parts - 1]] = jnp.where(left, refs[parts - 1][...], refs[parts][...])
        weights = joined[...].reshape(student.shape[1], BN)
        refs = refs[parts + 1 :]
    predicted = dot(weights, student[...])
    chosen, scale, weight = refs[:3]
    if first:
        error, loss, sums = refs[3:]
    else:
        loss_in, _, error, loss, sums = refs[3:]
    i = pl.program_id(0)

    @pl.when(i == 0)
    def _():
        sums[...] = jnp.zeros_like(sums) if first else loss_in[...]

    target = (chosen[...].astype(f32) - scale[:, 0:1]) * scale[:, 1:2]
    residual = predicted - target
    masked = weight[...] * residual
    error[...] = masked.astype(bf16)
    sums[...] += jnp.sum(masked * residual, axis=0, keepdims=True)

    @pl.when(i == steps - 1)
    def _():
        if first:
            loss[...] = sums[...]
        else:
            loss[...] = jnp.broadcast_to(jnp.sum(sums[...], axis=1, keepdims=True), loss.shape)


def product(student, weights, xs, chosen, scale, weight, start, before=None, copies=None):
    tokens, depth = student.shape
    parts = max(len(weights) - 1, 1)
    k = depth // parts
    cols = weights[0].shape[1]
    steps, at = cols // BN, start // BN
    first = before is None
    lefts = weights[-2].shape[1] // BN if parts > 1 else 0
    in_specs = [pl.BlockSpec(memory_space=pltpu.VMEM)]
    whole = len(weights) - 2 if parts > 1 else 1
    in_specs += [pl.BlockSpec((k, BN), lambda i, p: (0, i))] * whole
    if parts > 1:
        in_specs += [
            pl.BlockSpec((k, BN), lambda i, p: (0, jnp.minimum(i, lefts - 1))),
            pl.BlockSpec((k, BN), lambda i, p: (0, jnp.maximum(i - lefts, 0))),
        ]
    in_specs += [
        pl.BlockSpec((BN, tokens), lambda i, p: (i + at, 0)),
        pl.BlockSpec((BN, 2), lambda i, p: (i + at, 0)),
        pl.BlockSpec((1, tokens), lambda i, p: (0, 0)),
    ]
    args = [xs, student, *weights, stay(chosen), scale, weight]
    if not first:
        in_specs += [pl.BlockSpec((1, tokens), lambda i, p: (0, 0)), pl.BlockSpec(memory_space=pl.ANY)]
        args += list(before)
    loss = (1, tokens) if first else (copies, 128)
    return pl.pallas_call(
        lambda *refs: product_kernel(steps, parts, lefts, first, *refs),
        grid_spec=pltpu.PrefetchScalarGridSpec(
            num_scalar_prefetch=1,
            grid=(steps,),
            in_specs=in_specs,
            out_specs=[
                pl.BlockSpec((BN, tokens), lambda i, p: (i + at, 0)),
                pl.BlockSpec(loss, lambda i, p: (0, 0)),
            ],
            scratch_shapes=[pltpu.VMEM((1, tokens), f32)] + ([pltpu.VMEM((parts, k, BN), bf16)] if parts > 1 else []),
        ),
        out_shape=[
            jax.ShapeDtypeStruct(chosen.shape, bf16),
            jax.ShapeDtypeStruct(loss, f32),
        ],
        input_output_aliases={} if first else {len(args) - 1: 0},
        compiler_params=params(),
        cost_estimate=pl.CostEstimate(flops=2 * depth * cols * tokens, bytes_accessed=14_000_000, transcendentals=0),
        name="product",
    )(*args)


def after(value, *done):
    return lax.optimization_barrier((value, *done))[0]


def shards(teacher_states, student_states, projection, layer_pick, validity):
    z, x = lax.axis_index("seq_0"), lax.axis_index("seq_1")
    layers, rows, features = projection.shape
    tokens = student_states.shape[0]
    columns = layers * features

    mine = jnp.transpose(projection, (1, 0, 2)).reshape(rows, columns)
    c_mine, b_mine = mine[:, :C_COLS], mine[:, C_COLS:]

    c_next, c_last, c_far = from_x(c_mine, 1), from_x(c_mine, -1), from_x(c_mine, 2)
    line = {0: b_mine, 1: from_z(b_mine, 1), -1: from_z(b_mine, -1), 2: from_z(b_mine, 2), -2: from_z(b_mine, -2)}
    place = lax.broadcasted_iota(jnp.int32, (NX, 1, 1), 0)
    away = (place - x) % NX
    c_block = jnp.where(
        away == 0, c_mine[None], jnp.where(away == 1, c_next[None], jnp.where(away == 2, c_far[None], c_last[None]))
    ).reshape(NX * rows, C_COLS)
    line[3], line[-3], line[4] = from_z(line[2], 1), from_z(line[-2], -1), from_z(line[2], 2)

    weight = validity.astype(f32).reshape(1, tokens)
    chosen, stats = local_moments(
        jnp.transpose(teacher_states, (0, 2, 1)), after(weight, line[3], line[-3]), layer_pick
    )
    c_weights = lax.all_gather(after(c_block, *[line[k] for k in SC_AFTER]), "seq_0", axis=0, tiled=True)

    zs = (z + jnp.asarray(Z_ORDER, jnp.int32)) % NZ
    xs = (x + jnp.asarray(X_ORDER, jnp.int32)) % NX
    *line, zs, xs, stats = lax.optimization_barrier((*[line[k] for k in Z_ORDER], zs, xs, stats))

    own = placed(line, zs)
    x_after, x_before = from_x(own, 1), from_x(own, -1)
    student = by_x(after(student_states, own), rows)
    stats = merged([stats] + [from_x(stats, by) for by in (1, -1, 2)])
    stats = merged([stats] + [from_z(stats, by) for by in Z_ORDER[1:]])
    counted = stats[0, 2, 0]
    scale = jnp.stack(
        [stats[:, 0].reshape(columns), (1.0 / jnp.sqrt(stats[:, 1] / stats[:, 2] + epsilon)).reshape(columns)], axis=1
    )
    x_left, x_right = from_x(x_after[:, :HALF], 1), from_x(x_before[:, HALF:], -1)

    chosen = chosen.reshape(columns, tokens)
    copies = NZ * NX * lax.axis_size("feat_0") * lax.axis_size("feat_1")
    b_args = (student, [own, x_after, x_before, x_left, x_right], xs, chosen, scale, weight, C_COLS)
    c_args = (student_states, [stay(c_weights)], xs, chosen, scale, weight, 0)
    if C_FIRST:
        error, loss = product(*c_args)
        error, loss = product(*b_args, (loss, error), copies)
    else:
        error, loss = product(*b_args)
        error, loss = product(*c_args, (loss, error), copies)
    squares = jnp.sum(lax.all_to_all(loss, ALL, 0, 0, tiled=True)[:, 0])
    total_loss = squares / (counted * D * LAYERS)
    whitened = jnp.transpose(error.reshape(layers, features, tokens), (0, 2, 1))
    return whitened, total_loss


def solution(mesh):
    torus = Mesh(mesh.devices.reshape(NZ, NX, 4, 2), ALL)
    in_specs = (P(None, SEQ, FEAT), P(SEQ, None), P(None, SEQ, FEAT), P(), P(SEQ))
    out_specs = (P(None, SEQ, FEAT), P())
    return jax.shard_map(shards, mesh=torus, in_specs=in_specs, out_specs=out_specs, check_vma=False)
```

```python
import jax
import jax.numpy as jnp
from jax import lax
from jax.experimental import pallas as pl
from jax.experimental.pallas import tpu as pltpu
from jax.sharding import Mesh
from jax.sharding import PartitionSpec as P

D = 3584
LAYERS = 4
SEQ = ("seq_0", "seq_1")
FEAT = ("feat_0", "feat_1")
ALL = SEQ + FEAT
NZ, NX = 8, 4
epsilon = 1e-05

C_COLS = 768
HALF = 512
BN = 256
VMEM = 20 * 1024 * 1024
C_FIRST = True
SC_AFTER = (2, -2, 3, -3)

Z_ORDER = (0, 1, -1, 2, -2, 3, -3, 4)
X_ORDER = (0, 1, -1, 2)
f32 = jnp.float32
bf16 = jnp.bfloat16


def shift(value, axis, size, by):
    return lax.ppermute(value, axis, [(i, (i - by) % size) for i in range(size)])


def from_z(value, by):
    return shift(value, "seq_0", NZ, by)


def from_x(value, by):
    return shift(value, "seq_1", NX, by)


def params(**kw):
    return pltpu.CompilerParams(vmem_limit_bytes=VMEM, **kw)


def stay(value):
    return pltpu.with_memory_space_constraint(value, pltpu.HBM)


def moments_kernel(pick, teacher, weight, chosen, stats):
    x16 = teacher[0]
    chosen[0] = x16
    x = x16.astype(f32)
    w = weight[...]
    count = jnp.sum(w, axis=1, keepdims=True)
    mean = jnp.sum(x * w, axis=1, keepdims=True) / jnp.maximum(count, 1.0)
    centred = x - mean
    spread = jnp.sum(w * centred * centred, axis=1, keepdims=True)
    lane = lax.broadcasted_iota(jnp.int32, (x.shape[0], 128), 1)
    table = jnp.where(lane == 0, mean, jnp.where(lane == 1, spread, count))
    stats[0] = table.T[:8]


def local_moments(teacher, weight, pick):
    layers, features, tokens = teacher.shape
    return pl.pallas_call(
        moments_kernel,
        grid_spec=pltpu.PrefetchScalarGridSpec(
            num_scalar_prefetch=1,
            grid=(layers,),
            in_specs=[
                pl.BlockSpec((1, features, tokens), lambda i, p: (p[i], 0, 0)),
                pl.BlockSpec((1, tokens), lambda i, p: (0, 0)),
            ],
            out_specs=[
                pl.BlockSpec((1, features, tokens), lambda i, p: (i, 0, 0)),
                pl.BlockSpec((1, 8, features), lambda i, p: (i, 0, 0)),
            ],
        ),
        out_shape=[
            jax.ShapeDtypeStruct((layers, features, tokens), bf16),
            jax.ShapeDtypeStruct((layers, 8, features), f32),
        ],
        compiler_params=params(),
        cost_estimate=pl.CostEstimate(flops=20_000_000, bytes_accessed=8_000_000, transcendentals=0),
        name="moments",
    )(pick, stay(teacher), weight)


def merged(groups):
    mean, spread, count = ([g[:, k] for g in groups] for k in range(3))
    joined = sum(count)
    whole = jnp.maximum(joined, 1.0)
    middle = mean[0] + sum(n * (m - mean[0]) for m, n in zip(mean[1:], count[1:])) / whole
    around = sum(spread) + sum(n * (m - middle) * (m - middle) for m, n in zip(mean, count))
    row = lax.broadcasted_iota(jnp.int32, groups[0].shape, 1)
    return jnp.where(row == 0, middle[:, None], jnp.where(row == 1, around[:, None], joined[:, None]))


def place_kernel(zs, *refs):
    *pieces, out = refs
    for k, piece in enumerate(pieces):
        out[zs[k]] = piece[...]


def placed(pieces, zs):
    rows, cols = pieces[0].shape
    n = len(pieces)
    return pl.pallas_call(
        place_kernel,
        in_specs=[pl.BlockSpec(memory_space=pltpu.SMEM)] + [pl.BlockSpec(memory_space=pltpu.VMEM)] * n,
        out_specs=pl.BlockSpec(memory_space=pltpu.VMEM),
        out_shape=jax.ShapeDtypeStruct((n, rows, cols), bf16),
        compiler_params=params(),
        cost_estimate=pl.CostEstimate(flops=0, bytes_accessed=2_500_000, transcendentals=0),
        name="placed",
    )(zs, *pieces).reshape(n * rows, cols)


def columns_kernel(rows, student, out):
    order = [i * NX + j for j in range(NX) for i in range(NZ)]
    out[...] = jnp.concatenate([student[:, pl.ds(k * rows, rows)] for k in order], axis=1)


def by_x(student, rows):
    tokens, depth = student.shape
    block = 256
    return pl.pallas_call(
        lambda *refs: columns_kernel(rows, *refs),
        grid=(tokens // block,),
        in_specs=[pl.BlockSpec((block, depth), lambda i: (i, 0))],
        out_specs=pl.BlockSpec((block, depth), lambda i: (i, 0)),
        out_shape=jax.ShapeDtypeStruct((tokens, depth), bf16),
        compiler_params=params(),
        cost_estimate=pl.CostEstimate(flops=0, bytes_accessed=10_000_000, transcendentals=0),
        name="columns_by_x",
    )(student)


def dot(weights, student):
    return lax.dot_general(weights, student, (((0,), (1,)), ((), ())), preferred_element_type=f32)


def product_kernel(steps, parts, lefts, first, student, *refs):
    if parts == 1:
        weights = refs[0][...]
        refs = refs[1:]
    else:
        *refs, joined = refs
        x = lax.axis_index("seq_1")
        xs = [lax.rem(x + by + NX, NX) for by in X_ORDER]
        for k in range(parts - 1):
            joined[xs[k]] = refs[k][...]
        left = pl.program_id(0) < lefts
        joined[xs[parts - 1]] = jnp.where(left, refs[parts - 1][...], refs[parts][...])
        weights = joined[...].reshape(student.shape[1], BN)
        refs = refs[parts + 1 :]
    predicted = dot(weights, student[...])
    chosen, scale, weight = refs[:3]
    if first:
        error, loss, sums = refs[3:]
    else:
        loss_in, _, error, loss, sums = refs[3:]
    i = pl.program_id(0)

    @pl.when(i == 0)
    def _():
        sums[...] = jnp.zeros_like(sums) if first else loss_in[...]

    target = (chosen[...].astype(f32) - scale[:, 0:1]) * scale[:, 1:2]
    residual = predicted - target
    masked = weight[...] * residual
    error[...] = masked.astype(bf16)
    sums[...] += jnp.sum(masked * residual, axis=0, keepdims=True)

    @pl.when(i == steps - 1)
    def _():
        if first:
            loss[...] = sums[...]
        else:
            loss[...] = jnp.broadcast_to(jnp.sum(sums[...], axis=1, keepdims=True), loss.shape)


def product(student, weights, xs, chosen, scale, weight, start, before=None, copies=None):
    tokens, depth = student.shape
    parts = max(len(weights) - 1, 1)
    k = depth // parts
    cols = weights[0].shape[1]
    steps, at = cols // BN, start // BN
    first = before is None
    lefts = weights[-2].shape[1] // BN if parts > 1 else 0
    in_specs = [pl.BlockSpec(memory_space=pltpu.VMEM)]
    whole = len(weights) - 2 if parts > 1 else 1
    in_specs += [pl.BlockSpec((k, BN), lambda i: (0, i))] * whole
    if parts > 1:
        in_specs += [
            pl.BlockSpec((k, BN), lambda i: (0, jnp.minimum(i, lefts - 1))),
            pl.BlockSpec((k, BN), lambda i: (0, jnp.maximum(i - lefts, 0))),
        ]
    in_specs += [
        pl.BlockSpec((BN, tokens), lambda i: (i + at, 0)),
        pl.BlockSpec((BN, 2), lambda i: (i + at, 0)),
        pl.BlockSpec((1, tokens), lambda i: (0, 0)),
    ]
    args = [student, *weights, stay(chosen), scale, weight]
    if not first:
        in_specs += [pl.BlockSpec((1, tokens), lambda i: (0, 0)), pl.BlockSpec(memory_space=pl.ANY)]
        args += list(before)
    loss = (1, tokens) if first else (copies, 128)
    return pl.pallas_call(
        lambda *refs: product_kernel(steps, parts, lefts, first, *refs),
        grid_spec=pl.GridSpec(
            grid=(steps,),
            in_specs=in_specs,
            out_specs=[
                pl.BlockSpec((BN, tokens), lambda i: (i + at, 0)),
                pl.BlockSpec(loss, lambda i: (0, 0)),
            ],
            scratch_shapes=[pltpu.VMEM((1, tokens), f32)] + ([pltpu.VMEM((parts, k, BN), bf16)] if parts > 1 else []),
        ),
        out_shape=[
            jax.ShapeDtypeStruct(chosen.shape, bf16),
            jax.ShapeDtypeStruct(loss, f32),
        ],
        input_output_aliases={} if first else {len(args) - 1: 0},
        compiler_params=params(),
        cost_estimate=pl.CostEstimate(flops=2 * depth * cols * tokens, bytes_accessed=14_000_000, transcendentals=0),
        name="product",
    )(*args)


def after(value, *done):
    return lax.optimization_barrier((value, *done))[0]


def shards(teacher_states, student_states, projection, layer_pick, validity):
    z, x = lax.axis_index("seq_0"), lax.axis_index("seq_1")
    layers, rows, features = projection.shape
    tokens = student_states.shape[0]
    columns = layers * features

    mine = jnp.transpose(projection, (1, 0, 2)).reshape(rows, columns)
    c_mine, b_mine = mine[:, :C_COLS], mine[:, C_COLS:]

    c_next, c_last, c_far = from_x(c_mine, 1), from_x(c_mine, -1), from_x(c_mine, 2)
    line = {0: b_mine, 1: from_z(b_mine, 1), -1: from_z(b_mine, -1), 2: from_z(b_mine, 2), -2: from_z(b_mine, -2)}
    place = lax.broadcasted_iota(jnp.int32, (NX, 1, 1), 0)
    away = (place - x) % NX
    c_block = jnp.where(
        away == 0, c_mine[None], jnp.where(away == 1, c_next[None], jnp.where(away == 2, c_far[None], c_last[None]))
    ).reshape(NX * rows, C_COLS)
    line[3], line[-3], line[4] = from_z(line[2], 1), from_z(line[-2], -1), from_z(line[2], 2)

    weight = validity.astype(f32).reshape(1, tokens)
    chosen, stats = local_moments(
        jnp.transpose(teacher_states, (0, 2, 1)), after(weight, line[3], line[-3]), layer_pick
    )
    c_weights = lax.all_gather(after(c_block, *[line[k] for k in SC_AFTER]), "seq_0", axis=0, tiled=True)

    zs = (z + jnp.asarray(Z_ORDER, jnp.int32)) % NZ
    xs = (x + jnp.asarray(X_ORDER, jnp.int32)) % NX
    *line, zs, xs, stats = lax.optimization_barrier((*[line[k] for k in Z_ORDER], zs, xs, stats))

    own = placed(line, zs)
    x_after, x_before = from_x(own, 1), from_x(own, -1)
    student = by_x(after(student_states, own), rows)
    stats = merged([stats] + [from_x(stats, by) for by in (1, -1, 2)])
    stats = merged([stats] + [from_z(stats, by) for by in Z_ORDER[1:]])
    counted = stats[0, 2, 0]
    scale = jnp.stack(
        [stats[:, 0].reshape(columns), (1.0 / jnp.sqrt(stats[:, 1] / stats[:, 2] + epsilon)).reshape(columns)], axis=1
    )
    x_left, x_right = from_x(x_after[:, :HALF], 1), from_x(x_before[:, HALF:], -1)

    chosen = chosen.reshape(columns, tokens)
    copies = NZ * NX * lax.axis_size("feat_0") * lax.axis_size("feat_1")
    b_args = (student, [own, x_after, x_before, x_left, x_right], xs, chosen, scale, weight, C_COLS)
    c_args = (student_states, [stay(c_weights)], xs, chosen, scale, weight, 0)
    if C_FIRST:
        error, loss = product(*c_args)
        error, loss = product(*b_args, (loss, error), copies)
    else:
        error, loss = product(*b_args)
        error, loss = product(*c_args, (loss, error), copies)
    squares = jnp.sum(lax.all_to_all(loss, ALL, 0, 0, tiled=True)[:, 0])
    total_loss = squares / (counted * D * LAYERS)
    whitened = jnp.transpose(error.reshape(layers, features, tokens), (0, 2, 1))
    return whitened, total_loss


def solution(mesh):
    torus = Mesh(mesh.devices.reshape(NZ, NX, 4, 2), ALL)
    in_specs = (P(None, SEQ, FEAT), P(SEQ, None), P(None, SEQ, FEAT), P(), P(SEQ))
    out_specs = (P(None, SEQ, FEAT), P())
    return jax.shard_map(shards, mesh=torus, in_specs=in_specs, out_specs=out_specs, check_vma=False)
```
